512 devices in a mesh: img: 2 (over x_hi), row: 16 (over y, x_lo, core), col: 16 (over z).
Axes of the slice: x: 4 (x_hi: 2, x_lo: 2; x = x_hi * 2 + x_lo), y: 4, z: 16, core: 2. Of those that a mesh axis runs over, the one named last changes fastest.
Arguments:
- grid_elements: bfloat16 [1024, 512, 768], P(('img', 'row'), 'col'), parts along dimension 0, may hold values from -6 to 6
- summary_vectors: bfloat16 [64, 32, 768], P(('img', 'row'), 'col'), parts along dimension 0, may hold values from -6 to 6
- triple_projection: bfloat16 [768, 2304], P(None, 'row'), may hold values from -0.375 to 0.375
- final_projection: bfloat16 [768, 768], P(None, 'row'), may hold values from -0.21875 to 0.21875
- genuine_flags: int32 [1024, 512], P(('img', 'row'), 'col'), parts along dimension 0, may hold values 0 or 1
Outputs:
- element_result: bfloat16 [1024, 512, 768], P(('img', 'row'), 'col'), parts along dimension 0
- summary_result: bfloat16 [64, 32, 768], P(('img', 'row'), 'col'), parts along dimension 0
The draws below stay inside these ranges and needn't reach their ends.
There are 2 independent parts, one for each index of `img`. The reference program is written for one: setup_inputs(seed, part) draws one part's arguments, and reference() takes and returns one part's arrays. A program takes and returns all parts, laid end to end along the dimension named above; an argument that names none is the same for every part. Nothing has to cross between parts.
All inputs are finite; a program needn't handle non-finite values. No bound on the sum of `genuine_flags` on one device may be relied on, other than what follows from the above.
Results may differ from the reference program's by a relative error of at most 0.0096.
Values may be sent and summed in bfloat16 or wider, within the bound.
A program may use at most 64 MiB of HBM per device.

```python
import jax
import jax.numpy as jnp
from jax import lax

EMBED_SPAN = 768
HEAD_DIM = 64
HEADS = 12
PATCH_SIDE = 16
RADIUS = 4
GRID_TALL = 512
GRID_BROAD = 512
SUMMARY_TALL = 32
SUMMARY_BROAD = 32
KT = 24


def set_ends(drawn, key, smallest, top_value):
    shape = drawn.shape
    place = [jax.random.randint(jax.random.fold_in(key, axis), (), 0, shape[axis]) for axis in range(len(shape))]
    drawn = drawn.at[tuple(place)].set(smallest)
    longest = shape.index(max(shape))
    place[longest] = (place[longest] + 1) % shape[longest]
    return drawn.at[tuple(place)].set(top_value)


def shard_levels(rng, extent, pieces, smallest, top_value):
    loudness, own = 1.0, jax.random.fold_in(rng, 6)
    for position, shards_of in pieces:
        draws = jnp.exp(jax.random.uniform(jax.random.fold_in(own, position), (shards_of,), jnp.float32, smallest / len(pieces), top_value / len(pieces)))
        loudness = loudness * jnp.repeat(draws, extent[position] // shards_of).reshape([-1 if axis == position else 1 for axis in range(len(extent))])
    return loudness


def centred(key, dims, scale, most, pieces=(), held_as=jnp.bfloat16):
    drawn = jax.random.normal(key, dims, jnp.float32) * scale
    if len(pieces) > 0:
        drawn = shard_levels(key, dims, pieces, -0.22, 0.18) * drawn
    return jnp.clip(drawn, min=-most, max=most).astype(held_as)


def setup_inputs(seed: int = 0, part: int = 0) -> dict:
    streams_of = jax.random.split(jax.random.key(seed), 6)
    own_keys = jax.random.split(jax.random.fold_in(streams_of[5], part), 6)
    grid_elements = centred(own_keys[0], (GRID_TALL, GRID_BROAD, EMBED_SPAN), 1.0, 6.0, ((0, 16), (1, 16)))
    summary_vectors = centred(own_keys[1], (SUMMARY_TALL, SUMMARY_BROAD, EMBED_SPAN), 1.0, 6.0, ((0, 16), (1, 16)))
    triple_projection = centred(streams_of[2], (EMBED_SPAN, 3 * EMBED_SPAN), (EMBED_SPAN // 3) ** -0.5, 0.375, ((1, 16),))
    final_projection = centred(streams_of[3], (EMBED_SPAN, EMBED_SPAN), EMBED_SPAN ** -0.5, 0.21875, ((1, 16),))
    genuine_flags = set_ends((jax.random.randint(own_keys[4], (GRID_TALL, GRID_BROAD), 0, 4) < 3).astype(jnp.int32), jax.random.fold_in(own_keys[4], 1), 0, 1)
    return {"grid_elements": grid_elements, "summary_vectors": summary_vectors, "triple_projection": triple_projection, "final_projection": final_projection, "genuine_flags": genuine_flags}


def layer_normalise(payload_lines):
    payload_lines = payload_lines.astype(jnp.float32)
    center = payload_lines - lax.optimization_barrier(jnp.mean(payload_lines, axis=-1, keepdims=True))
    spread = lax.optimization_barrier(jnp.mean(center * center, axis=-1, keepdims=True))
    return center * lax.rsqrt(spread + 1e-05)

def summary_attention(asking_lines, lookup_lines, payload_lines, attention_branches, logit_factor):
    query_count = asking_lines.shape[0]
    key_count = lookup_lines.shape[0]
    asking_branches = asking_lines.astype(jnp.float32).reshape(query_count, attention_branches, -1)
    k_heads = lookup_lines.astype(jnp.float32).reshape(key_count, attention_branches, -1)
    v_heads = payload_lines.astype(jnp.float32).reshape(key_count, attention_branches, -1)
    scores = jnp.einsum('qhd,khd->hqk', asking_branches, k_heads) * logit_factor
    logit_exponential = jnp.exp(scores)
    weights = (logit_exponential / lax.optimization_barrier(jnp.sum(logit_exponential, axis=-1, keepdims=True))).astype(jnp.bfloat16)
    blended_channels = jnp.einsum('hqk,khd->qhd', weights.astype(jnp.float32), v_heads)
    return blended_channels.reshape(query_count, -1).astype(jnp.bfloat16)

def band_mask(window_side, tile_side, reach):
    query_pos = jnp.arange(window_side * window_side, dtype=jnp.int32)
    key_pos = jnp.arange(tile_side * tile_side, dtype=jnp.int32)
    row_step = key_pos[None, :] // tile_side - query_pos[:, None] // window_side
    col_step = key_pos[None, :] % tile_side - query_pos[:, None] % window_side
    return (row_step >= 0) & (row_step <= 2 * reach) & (col_step >= 0) & (col_step <= 2 * reach)

def local_attention(asking_lines, lookup_lines, payload_lines, visibility_matrix, summary_lookup, summary_payload, attention_branches, logit_factor):
    query_count = asking_lines.shape[0]
    key_count = lookup_lines.shape[0]
    asking_branches = asking_lines.astype(jnp.float32).reshape(query_count, attention_branches, -1)
    k_heads = lookup_lines.astype(jnp.float32).reshape(key_count, attention_branches, -1)
    v_heads = payload_lines.astype(jnp.float32).reshape(key_count, attention_branches, -1)
    summary_lookup_lines = summary_lookup.astype(jnp.float32).reshape(attention_branches, -1)
    summary_payload_lines = summary_payload.astype(jnp.float32).reshape(attention_branches, -1)
    scores = jnp.einsum('qhd,khd->hqk', asking_branches, k_heads) * logit_factor
    summary_logits = jnp.einsum('zry,ry->rz', asking_branches, summary_lookup_lines) * logit_factor
    logit_exponential = jnp.where(visibility_matrix[None, :, :], jnp.exp(scores), 0.0)
    summary_exponential = jnp.exp(summary_logits)
    normaliser_total = lax.optimization_barrier(jnp.sum(logit_exponential, axis=-1)) + summary_exponential
    weights = (logit_exponential / normaliser_total[:, :, None]).astype(jnp.bfloat16)
    summary_attention_dist = (summary_exponential / normaliser_total).astype(jnp.bfloat16)
    blended_channels = jnp.einsum('hqk,khd->qhd', weights.astype(jnp.float32), v_heads)
    blended_channels = blended_channels + jnp.einsum('qh,qv->hqv', summary_attention_dist.astype(jnp.float32), summary_payload_lines)
    return blended_channels.reshape(query_count, -1).astype(jnp.bfloat16)

def reference(grid_elements, summary_vectors, triple_projection, final_projection, genuine_flags):
    attention_branches = HEADS
    logit_factor = HEAD_DIM ** (-0.5)
    summary_sequence = summary_vectors.reshape(SUMMARY_TALL * SUMMARY_BROAD, EMBED_SPAN)
    summary_gain_vector = layer_normalise(summary_sequence).astype(jnp.bfloat16)
    summary_projected_triple = jnp.dot(summary_gain_vector, triple_projection, preferred_element_type=jnp.float32).astype(jnp.bfloat16)
    blended_summaries = summary_attention(summary_projected_triple[:, :EMBED_SPAN], summary_projected_triple[:, EMBED_SPAN:2 * EMBED_SPAN], summary_projected_triple[:, 2 * EMBED_SPAN:], attention_branches, logit_factor)
    renewed_summaries = summary_sequence.astype(jnp.float32) + jnp.dot(blended_summaries, final_projection, preferred_element_type=jnp.float32)
    summary_result = renewed_summaries.astype(jnp.bfloat16).reshape(SUMMARY_TALL, SUMMARY_BROAD, EMBED_SPAN)
    summary_lookup_payload = jnp.dot(layer_normalise(renewed_summaries).astype(jnp.bfloat16), triple_projection[:, EMBED_SPAN:], preferred_element_type=jnp.float32).astype(jnp.bfloat16)
    token_norm = layer_normalise(grid_elements.reshape(GRID_TALL * GRID_BROAD, EMBED_SPAN)).astype(jnp.bfloat16)
    token_qkv = jnp.dot(token_norm, triple_projection, preferred_element_type=jnp.float32).astype(jnp.bfloat16).reshape(GRID_TALL, GRID_BROAD, 3 * EMBED_SPAN)
    padded_kv = jnp.pad(token_qkv[:, :, EMBED_SPAN:], ((RADIUS, RADIUS), (RADIUS, RADIUS), (0, 0)))
    padded_valid = jnp.pad(genuine_flags, ((RADIUS, RADIUS), (RADIUS, RADIUS)))
    allowed_band = band_mask(PATCH_SIDE, KT, RADIUS)
    zero_index = jnp.zeros((), jnp.int32)

    def single_patch(patch_position):
        patch_line = (patch_position // SUMMARY_BROAD).astype(jnp.int32) * PATCH_SIDE
        patch_column = (patch_position % SUMMARY_BROAD).astype(jnp.int32) * PATCH_SIDE
        asking_lines = lax.dynamic_slice(token_qkv, (patch_line, patch_column, zero_index), (PATCH_SIDE, PATCH_SIDE, EMBED_SPAN)).reshape(PATCH_SIDE * PATCH_SIDE, EMBED_SPAN)
        patch_lookups = lax.dynamic_slice(padded_kv, (patch_line, patch_column, zero_index), (KT, KT, 2 * EMBED_SPAN)).reshape(KT * KT, 2 * EMBED_SPAN)
        usable = lax.dynamic_slice(padded_valid, (patch_line, patch_column), (KT, KT)).reshape(KT * KT)
        visibility_matrix = allowed_band & (usable[None, :] > 0)
        summary_line = summary_lookup_payload[patch_position]
        return local_attention(asking_lines, patch_lookups[:, :EMBED_SPAN], patch_lookups[:, EMBED_SPAN:], visibility_matrix, summary_line[:EMBED_SPAN], summary_line[EMBED_SPAN:], attention_branches, logit_factor)
    blended_channels = lax.map(single_patch, jnp.arange(SUMMARY_TALL * SUMMARY_BROAD, dtype=jnp.int32))
    blended_channels = blended_channels.reshape(SUMMARY_TALL, SUMMARY_BROAD, PATCH_SIDE, PATCH_SIDE, EMBED_SPAN).transpose(0, 2, 1, 3, 4).reshape(GRID_TALL * GRID_BROAD, EMBED_SPAN)
    tokens_new = grid_elements.reshape(GRID_TALL * GRID_BROAD, EMBED_SPAN).astype(jnp.float32) + jnp.dot(blended_channels, final_projection, preferred_element_type=jnp.float32)
    element_result = tokens_new.astype(jnp.bfloat16).reshape(GRID_TALL, GRID_BROAD, EMBED_SPAN)
    return (element_result, summary_result)
```

```python
import functools
import math

import jax
import jax.numpy as jnp
from jax import lax
from jax.experimental import pallas as pl
from jax.experimental.pallas import tpu as pltpu
from jax.sharding import PartitionSpec as P

MESH = pl.DeviceIdType.MESH
D = 768
HEADS = 12
PAIRS = HEADS // 2
TOK = 1024
CEN = 1280
SIDE = 160
KEYS = CEN + 2 * SIDE
PIECE = 48
F32 = jnp.float32
BF = jnp.bfloat16
NT = (((1,), (1,)), ((), ()))
Q_SCALE = 0.125 * math.log2(math.e)
MASKED = -1e30


def nt(a, b):
    return lax.dot_general(a, b, NT, preferred_element_type=F32)


def nn(a, b):
    return jnp.dot(a, b, preferred_element_type=F32)


def layer_norm(v):
    center = v - jnp.mean(v, axis=-1, keepdims=True)
    spread = jnp.mean(center * center, axis=-1, keepdims=True)
    return center * lax.rsqrt(spread + 1e-05)


def iota(shape, dim):
    return lax.broadcasted_iota(jnp.int32, shape, dim)


def rows(start, size):
    return pl.ds(pl.multiple_of(start, 16), size)


def kernel(
    x_hbm,
    sv_hbm,
    w_hbm,
    wf_hbm,
    fl_hbm,
    out_hbm,
    sr_hbm,
    xraw,
    edge,
    side,
    xq,
    xkv,
    w_v,
    wf_v,
    wt,
    wft,
    flb,
    vb,
    svz,
    svr,
    cst,
    xc,
    qkvc,
    osc,
    sbuf,
    rbuf,
    wsc,
    csc,
    sr_v,
    kc,
    vc,
    q_s,
    k_s,
    v_s,
    bias,
    mix,
    obuf,
    load_sem,
    halo_s,
    halo_r,
    flag_s,
    flag_r,
    y_s,
    y_r,
    x_s,
    x_r,
    d_s,
    d_r,
    cz_s,
    cz_r,
    cr_s,
    cr_r,
    p_s,
    p_r,
    o_s,
):
    img = lax.axis_index("img")
    r = lax.axis_index("row")
    c = lax.axis_index("col")
    y = r // 4
    xl = (r // 2) % 2
    core = r % 2
    d = 1 - 2 * core
    x = img * 2 + xl
    up, down = (r + 15) % 16, (r + 1) % 16
    left, right = (c + 15) % 16, (c + 1) % 16
    xn = (x + d + 4) % 4
    dev_y = (img, ((y + d + 4) % 4) * 4 + xl * 2 + core, c)
    dev_x = (xn // 2, y * 4 + (xn % 2) * 2 + core, c)
    dev_p = (img, y * 4 + xl * 2 + (1 - core), c)
    cross = (1 - img, y * 4 + (1 - xl) * 2 + core, c)

    def local(src, dst, i):
        return pltpu.make_async_copy(src, dst, load_sem.at[i])

    def remote(src, dst, s, t, dev):
        return pltpu.make_async_remote_copy(
            src_ref=src, dst_ref=dst, send_sem=s, recv_sem=t, device_id=dev, device_id_type=MESH
        )

    ld_x = local(x_hbm, xraw.at[pl.ds(128, TOK)], 0)
    ld_w = local(w_hbm, w_v, 1)
    ld_wf = local(wf_hbm, wf_v, 2)
    ld_f = local(fl_hbm, flb.at[4], 3)
    ld_z = local(sv_hbm, svz.at[c], 4)
    ld_r = local(sv_hbm, svr.at[r], 5)
    for cp in (ld_w, ld_wf, ld_x, ld_f, ld_z, ld_r):
        cp.start()

    barrier = pltpu.get_barrier_semaphore()

    def greet(dev):
        pl.semaphore_signal(barrier, inc=1, device_id=dev, device_id_type=MESH)

    for i in range(1, 16):
        greet((img, r, (c + i) % 16))
    for i in range(1, 16):
        greet((img, (r + i) % 16, c))
    for rr in (up, down):
        for cc in (left, right):
            greet((img, rr, cc))
    greet(cross)

    def eye(n):
        return (iota((n, n), 0) == iota((n, n), 1)).astype(BF)

    ld_w.wait()
    wt[rows(r * 144, 144)] = nt(eye(144), w_v[...]).astype(BF)
    ld_wf.wait()
    wft[rows(r * PIECE, PIECE)] = nt(eye(PIECE), wf_v[...]).astype(BF)

    ld_x.wait()
    pick = iota((64, 256), 0)
    at = (pick % 32) // 4 * 32 + pick % 4 + (pick // 32) * 28
    pick = (iota((64, 256), 1) == at).astype(BF)
    for g in range(4):
        both = nn(pick, xraw[128 + 256 * g : 384 + 256 * g]).astype(BF)
        edge[32 * g : 32 * g + 32] = both[:32]
        edge[128 + 32 * g : 160 + 32 * g] = both[32:]

    pl.semaphore_wait(barrier, 35)

    def piece(rr, p):
        if p < 3:
            return wt.at[rows(rr * 144 + PIECE * p, PIECE)]
        return wft.at[rows(rr * PIECE, PIECE)]

    def y_copy(s, p, origin):
        return remote(piece(origin, p), piece(origin, p), y_s.at[s, p], y_r.at[s, p], dev_y)

    def x_copy(s, p, origin):
        return remote(piece(origin, p), piece(origin, p), x_s.at[s, p], x_r.at[s, p], dev_x)

    def d_copy(j, p, origin):
        return remote(piece(origin, p), piece(origin, p), d_s.at[j, p], d_r.at[j, p], dev_p)

    def mine(j):
        return ((y - j * d + 8) % 4) * 4 + xl * 2 + core

    def other(j):
        return ((y - j * d + 8) % 4) * 4 + (1 - xl) * 2 + core

    def partner(j):
        return ((y + j % 4 * d + 8) % 4) * 4 + (xl if j < 4 else 1 - xl) * 2 + (1 - core)

    def send_own(p):
        y_copy(0, p, mine(0)).start()
        x_copy(0, p, mine(0)).start()
        d_copy(0, p, mine(0)).start()

    def on_y(s, p):
        y_copy(s, p, mine(s + 1)).wait_recv()
        if s < 2:
            y_copy(s + 1, p, mine(s + 1)).start()
        x_copy(s + 1, p, mine(s + 1)).start()
        d_copy(s + 1, p, mine(s + 1)).start()

    def on_x(s, p):
        x_copy(s, p, other(s)).wait_recv()
        d_copy(4 + s, p, other(s)).start()

    for p in range(3):
        send_own(p)

    def halo(i, src, dst, dev):
        return remote(src, dst, halo_s.at[i], halo_r.at[i], dev)

    e_l, e_r = 0, 128
    halos = [
        halo(0, x_hbm.at[pl.ds(0, 128)], xraw.at[pl.ds(1152, 128)], (img, up, c)),
        halo(1, x_hbm.at[pl.ds(896, 128)], xraw.at[pl.ds(0, 128)], (img, down, c)),
        halo(2, edge.at[pl.ds(e_l, 128)], side.at[1, pl.ds(16, 128)], (img, r, left)),
        halo(3, edge.at[pl.ds(e_r, 128)], side.at[0, pl.ds(16, 128)], (img, r, right)),
        halo(4, edge.at[pl.ds(e_l, 16)], side.at[1, pl.ds(144, 16)], (img, up, left)),
        halo(5, edge.at[pl.ds(e_r, 16)], side.at[0, pl.ds(144, 16)], (img, up, right)),
        halo(6, edge.at[pl.ds(e_l + 112, 16)], side.at[1, pl.ds(0, 16)], (img, down, left)),
        halo(7, edge.at[pl.ds(e_r + 112, 16)], side.at[0, pl.ds(0, 16)], (img, down, right)),
    ]
    for cp in halos:
        cp.start()
    flags = []
    for dy, rr in ((-1, up), (0, r), (1, down)):
        for dx, cc in ((-1, left), (0, c), (1, right)):
            if dy or dx:
                to = (1 - dy) * 3 + (1 - dx)
                flags.append(remote(fl_hbm, flb.at[to], flag_s.at[to], flag_r.at[to], (img, rr, cc)))
    for cp in flags:
        cp.start()
    carriers = []
    for i in range(1, 16):
        dev = (img, r, (c + i) % 16)
        carriers.append(remote(sv_hbm, svz.at[c], cz_s.at[i], cz_r.at[i], dev))
        dev = (img, (r + i) % 16, c)
        carriers.append(remote(sv_hbm, svr.at[r], cr_s.at[i], cr_r.at[i], dev))
    for cp in carriers:
        cp.start()

    ones32 = jnp.ones((32, 128), BF)
    diag = (iota((32, 32), 0) == iota((32, 32), 1)).astype(F32)
    keep_up = jnp.where(r > 0, 1.0, 0.0)
    keep_down = jnp.where(r < 15, 1.0, 0.0)
    keep_left = jnp.where(c > 0, 1.0, 0.0)
    keep_right = jnp.where(c < 15, 1.0, 0.0)

    def group(g, dx):
        slot, at, keep = 1, 4 * (g - 1), 1.0
        if g == 0:
            slot, at, keep = 0, 28, keep_up
        if g == 9:
            slot, at, keep = 2, 0, keep_down
        return flb[slot * 3 + 1 + dx][at : at + 4].astype(F32) * keep

    def center_flags(g):
        f = group(g, 0)
        spread = [jnp.broadcast_to(f[i : i + 1], (32, 32)) * diag for i in range(4)]
        spread = jnp.concatenate(spread, axis=0).astype(BF)
        vb[128 * g : 128 * g + 128] = nn(spread, ones32).astype(BF)

    def side_flags(g, dx):
        f = group(g, dx) * (keep_left if dx < 0 else keep_right)
        p = iota((16, 32), 0)
        lane = p % 4 + (28 if dx < 0 else 0)
        spread = jnp.zeros((16, 32), F32)
        for i in range(4):
            spread = spread + jnp.where(p // 4 == i, jnp.broadcast_to(f[i : i + 1], (16, 32)), 0.0)
        spread = jnp.where(iota((16, 32), 1) == lane, spread, 0.0).astype(BF)
        start = CEN + (0 if dx < 0 else SIDE) + 16 * g
        vb[start : start + 16] = nn(spread, ones32).astype(BF)

    def norm_block(ref, src, dst, n, own):
        def body(i, carry):
            normed = layer_norm(ref[rows(src + 32 * i, 32)].astype(F32))
            if own is not None:
                xq[rows(own + 32 * i, 32)] = normed.astype(BF)
            mask = vb[rows(dst + 32 * i, 32)].astype(F32)
            xkv[rows(dst + 32 * i, 32)] = (normed * jnp.concatenate([mask] * 6, axis=1)).astype(BF)
            return carry

        lax.fori_loop(0, n // 32, body, 0)

    ld_f.wait()
    for g in range(1, 9):
        center_flags(g)

    def own_norm(i):
        norm_block(xraw, 128 + 128 * i, 128 + 128 * i, 128, 128 * i)

    own_norm(0)
    step = 1
    for s in range(2):
        for p in range(3):
            on_y(s, p)
            on_x(s, p)
            if s == 0 and p == 2:
                send_own(3)
            if step < 8:
                own_norm(step)
                step += 1
    while step < 8:
        own_norm(step)
        step += 1

    for cp in halos:
        cp.wait_recv()
    for cp in flags:
        cp.wait_recv()
    for g in (0, 9):
        center_flags(g)
    for g in range(10):
        side_flags(g, -1)
        side_flags(g, 1)
    norm_block(xraw, 0, 0, 128, None)
    norm_block(xraw, 1152, 1152, 128, None)
    for p in range(3):
        on_y(2, p)
        on_x(2, p)
    norm_block(side.at[0], 0, CEN, SIDE, None)
    norm_block(side.at[1], 0, CEN + SIDE, SIDE, None)
    for p in range(3):
        on_x(3, p)

    ld_z.wait()
    ld_r.wait()
    for cp in carriers:
        cp.wait_recv()
    for p in range(16):
        for i in range(2):
            cst[4 * p + 2 * i : 4 * p + 2 * i + 2] = svz[p, i].astype(F32)
            cst[64 + 4 * p + 2 * i : 66 + 4 * p + 2 * i] = svr[p, i].astype(F32)
    for i in range(4):
        xc[32 * i : 32 * i + 32] = layer_norm(cst[32 * i : 32 * i + 32]).astype(BF)

    qi = iota((256, 512), 0) % 128
    ki = iota((256, 512), 1)
    q_row, q_col = qi // 32, qi % 32
    in_side = ki >= 384
    k2 = jnp.where(ki >= 432, ki - 432, ki - 384)
    k_row = jnp.where(in_side, k2 // 4, ki // 32)
    k_col = jnp.where(in_side, k2 % 4 + jnp.where(ki >= 432, 36, 0), ki % 32 + 4)
    dr, dc = k_row - q_row, k_col - q_col
    near = (ki < 480) & (dr >= 0) & (dr <= 8) & (dc >= 0) & (dc <= 8)
    for wr in range(2):
        seen = near | (ki == 480 + wr * 2 + q_col // 16)
        bias[wr] = jnp.where(seen, 0.0, MASKED)

    for j in range(8):
        for p in range(3):
            d_copy(j, p, partner(j)).wait_recv()

    for s in range(3):
        on_y(s, 3)
        on_x(s, 3)

    def carrier_qkv(n, carry):
        got = nt(xc[...], wt[rows(n * 256, 256)])
        qkvc[:, pl.ds(pl.multiple_of(n * 256, 256), 256)] = got.astype(BF)
        return carry

    lax.fori_loop(0, 9, carrier_qkv, 0)
    low = iota((64, 128), 1) < 64
    lane64 = iota((64, 128), 1)
    zero = jnp.zeros((64, 128), BF)
    m_stat = jnp.zeros((64, 128), F32)
    l_stat = jnp.ones((64, 128), F32)
    for j in range(PAIRS):
        qp = qkvc[64:128, 128 * j : 128 * j + 128]
        kp = qkvc[0:64, D + 128 * j : D + 128 * j + 128]
        vp = qkvc[0:64, 2 * D + 128 * j : 2 * D + 128 * j + 128]
        qs = jnp.concatenate([jnp.where(low, qp, zero), jnp.where(low, zero, qp)], axis=0)
        sc = nt(qs, kp) * 0.125
        m = jnp.max(sc, axis=-1, keepdims=True)
        e = jnp.exp(sc - m)
        l = jnp.sum(e, axis=-1, keepdims=True)
        o = nn(e.astype(BF), vp) / l
        osc[:, 128 * j : 128 * j + 128] = jnp.where(low, o[:64], o[64:])
        for k in range(2):
            m_stat = jnp.where(lane64 == 2 * j + k, m[64 * k : 64 * k + 64], m_stat)
            l_stat = jnp.where(lane64 == 2 * j + k, l[64 * k : 64 * k + 64], l_stat)
    osc[:, D : D + 128] = m_stat
    osc[:, D + 128 : D + 256] = l_stat
    for p in range(16):
        sbuf[p] = osc[4 * p : 4 * p + 4]
    rbuf[r] = sbuf[r]
    parts = []
    for i in range(1, 16):
        to = (r + i) % 16
        parts.append(remote(sbuf.at[to], rbuf.at[r], p_s.at[i], p_r.at[i], (img, to, c)))
    for cp in parts:
        cp.start()

    def token_q(n, carry):
        wide = pl.ds(pl.multiple_of(n * 256, 256), 256)
        w_n = wt[rows(n * 256, 256)]
        for i in range(4):
            got = nt(xq[256 * i : 256 * i + 256], w_n)
            q_s[256 * i : 256 * i + 256, wide] = (got * Q_SCALE).astype(BF)
        return carry

    lax.fori_loop(0, 3, token_q, 0)

    def token_kv(n, carry):
        wide = pl.ds(pl.multiple_of(n * 256, 256), 256)
        w_k = wt[rows(D + n * 256, 256)]
        w_w = wt[rows(2 * D + n * 256, 256)]
        for i in range(4):
            k_s[400 * i : 400 * i + 400, wide] = nt(xkv[400 * i : 400 * i + 400], w_k).astype(BF)
        for i in range(4):
            v_s[400 * i : 400 * i + 400, wide] = nt(xkv[400 * i : 400 * i + 400], w_w).astype(BF)
        return carry

    lax.fori_loop(0, 3, token_kv, 0)

    for p in range(1):
        on_x(3, 3)
    for j in range(8):
        d_copy(j, 3, partner(j)).wait_recv()

    for cp in parts:
        cp.wait_recv()
    top = rbuf[0, :, D : D + 128]
    for p in range(1, 16):
        top = jnp.maximum(top, rbuf[p, :, D : D + 128])
    total = jnp.zeros((4, 128), F32)
    for p in range(16):
        total = total + jnp.exp(rbuf[p, :, D : D + 128] - top) * rbuf[p, :, D + 128 : D + 256]
    for p in range(16):
        share = jnp.exp(rbuf[p, :, D : D + 128] - top) * rbuf[p, :, D + 128 : D + 256]
        wsc[4 * p : 4 * p + 4] = share / total
    widen = (iota((128, D), 0) == iota((128, D), 1) // 64).astype(F32)
    wide_share = jnp.dot(
        wsc[...], widen, preferred_element_type=F32, precision=lax.Precision.HIGHEST
    )
    joined = jnp.zeros((4, D), F32)
    for p in range(16):
        joined = joined + wide_share[4 * p : 4 * p + 4] * rbuf[p, :, 0:D]
    csc[...] = jnp.zeros((2, 32, D), F32)
    csc[0, 0:4] = joined
    csc[1, 0:2] = svr[r, 0].astype(F32)
    csc[1, 2:4] = svr[r, 1].astype(F32)
    renewed = csc[1] + nt(csc[0].astype(BF), wft[...])
    sr_v[0] = renewed[0:2].astype(BF)
    sr_v[1] = renewed[2:4].astype(BF)
    st_sr = pltpu.make_async_copy(sr_v, sr_hbm, load_sem.at[6])
    st_sr.start()
    again = layer_norm(renewed).astype(BF)
    kc[...] = nt(again, wt[D : 2 * D]).astype(BF)
    vc[...] = nt(again, wt[2 * D : 3 * D]).astype(BF)

    low128 = iota((128, 128), 1) < 64
    zero128 = jnp.zeros((128, 128), BF)
    ones_c = jnp.ones((32, 128), BF)

    def tile(t, carry):
        cen = rows(128 * t, 384)
        lef = rows(CEN + 16 * t, 48)
        rig = rows(CEN + SIDE + 16 * t, 48)
        here = rows(128 * t, 128)
        seen = bias.at[t // 4]
        vbt = jnp.concatenate([vb[cen], vb[lef], vb[rig], ones_c], axis=0)
        for j in range(PAIRS):
            ln = pl.ds(128 * j, 128)
            kt = jnp.concatenate([k_s[cen, ln], k_s[lef, ln], k_s[rig, ln], kc[:, ln]], axis=0)
            vt = jnp.concatenate([v_s[cen, ln], v_s[lef, ln], v_s[rig, ln], vc[:, ln]], axis=0)
            qp = q_s[here, ln]
            qs = jnp.concatenate(
                [jnp.where(low128, qp, zero128), jnp.where(low128, zero128, qp)], axis=0
            )
            sc = nt(qs, kt) + seen[...]
            m = jnp.max(sc, axis=-1, keepdims=True)
            e = jnp.exp2(sc - m).astype(BF)
            o = nn(e, jnp.concatenate([vt, vbt], axis=1))
            o = o[:, :128] / o[:, 128:]
            mix[here, ln] = jnp.where(low128, o[:128], o[128:]).astype(BF)
        return carry

    lax.fori_loop(0, 8, tile, 0)

    outs = []
    for i in range(4):
        mine_rows = pl.ds(256 * i, 256)
        added = nt(mix[256 * i : 256 * i + 256], wft[...])
        got = xraw[128 + 256 * i : 384 + 256 * i].astype(F32) + added
        obuf[i] = got.astype(BF)
        cp = pltpu.make_async_copy(obuf.at[i], out_hbm.at[mine_rows], o_s.at[i])
        cp.start()
        outs.append(cp)

    for cp in outs:
        cp.wait()
    st_sr.wait()
    for cp in halos + flags + carriers + parts:
        cp.wait_send()
    for p in range(4):
        for s in range(3):
            y_copy(s, p, mine(s)).wait_send()
        for s in range(4):
            x_copy(s, p, mine(s)).wait_send()
            d_copy(s, p, mine(s)).wait_send()
            d_copy(4 + s, p, other(s)).wait_send()


def local(grid_elements, summary_vectors, triple_projection, final_projection, genuine_flags):
    any_spec = pl.BlockSpec(memory_space=pl.ANY)
    dma = pltpu.SemaphoreType.DMA
    out, summary = pl.pallas_call(
        kernel,
        out_shape=(
            jax.ShapeDtypeStruct((TOK, D), BF),
            jax.ShapeDtypeStruct((2, 2, D), BF),
        ),
        in_specs=[any_spec] * 5,
        out_specs=(any_spec, any_spec),
        scratch_shapes=[
            pltpu.VMEM((CEN, D), BF),
            pltpu.VMEM((256, D), BF),
            pltpu.VMEM((2, SIDE, D), BF),
            pltpu.VMEM((TOK, D), BF),
            pltpu.VMEM((KEYS, D), BF),
            pltpu.VMEM((D, 144), BF),
            pltpu.VMEM((D, 48), BF),
            pltpu.VMEM((3 * D, D), BF),
            pltpu.VMEM((D, D), BF),
            pltpu.VMEM((9, 32, 32), jnp.int32),
            pltpu.VMEM((KEYS, 128), BF),
            pltpu.VMEM((16, 2, 2, D), BF),
            pltpu.VMEM((16, 2, 2, D), BF),
            pltpu.VMEM((128, D), F32),
            pltpu.VMEM((128, D), BF),
            pltpu.VMEM((128, 3 * D), BF),
            pltpu.VMEM((64, 1024), F32),
            pltpu.VMEM((16, 4, 1024), F32),
            pltpu.VMEM((16, 4, 1024), F32),
            pltpu.VMEM((64, 128), F32),
            pltpu.VMEM((2, 32, D), F32),
            pltpu.VMEM((2, 2, D), BF),
            pltpu.VMEM((32, D), BF),
            pltpu.VMEM((32, D), BF),
            pltpu.VMEM((TOK, D), BF),
            pltpu.VMEM((KEYS, D), BF),
            pltpu.VMEM((KEYS, D), BF),
            pltpu.VMEM((2, 256, 512), F32),
            pltpu.VMEM((TOK, D), BF),
            pltpu.VMEM((4, 256, D), BF),
            dma((7,)),
            dma((8,)),
            dma((8,)),
            dma((9,)),
            dma((9,)),
            dma((3, 4)),
            dma((3, 4)),
            dma((4, 4)),
            dma((4, 4)),
            dma((8, 4)),
            dma((8, 4)),
            dma((16,)),
            dma((16,)),
            dma((16,)),
            dma((16,)),
            dma((16,)),
            dma((16,)),
            dma((4,)),
        ],
        compiler_params=pltpu.CompilerParams(
            collective_id=0, has_side_effects=True, vmem_limit_bytes=60 * 1024 * 1024
        ),
        name="block",
    )(
        grid_elements.reshape(TOK, D),
        summary_vectors,
        triple_projection,
        final_projection,
        genuine_flags,
    )
    return out.reshape(grid_elements.shape), summary


def solution(mesh):
    placed = (
        P(("img", "row"), "col", None),
        P(("img", "row"), "col", None),
        P(None, "row"),
        P(None, "row"),
        P(("img", "row"), "col"),
    )
    return jax.shard_map(
        local,
        mesh=mesh,
        in_specs=placed,
        out_specs=(P(("img", "row"), "col", None), P(("img", "row"), "col", None)),
        check_vma=False,
    )
```

```python
import functools
import math

import jax
import jax.numpy as jnp
from jax import lax
from jax.experimental import pallas as pl
from jax.experimental.pallas import tpu as pltpu
from jax.sharding import PartitionSpec as P

MESH = pl.DeviceIdType.MESH
D = 768
HEADS = 12
PAIRS = HEADS // 2
TOK = 1024
CEN = 1280
SIDE = 160
KEYS = CEN + 2 * SIDE
PIECE = 48
F32 = jnp.float32
BF = jnp.bfloat16
NT = (((1,), (1,)), ((), ()))
Q_SCALE = 0.125 * math.log2(math.e)
MASKED = -1e30


def nt(a, b):
    return lax.dot_general(a, b, NT, preferred_element_type=F32)


def nn(a, b):
    return jnp.dot(a, b, preferred_element_type=F32)


def layer_norm(v):
    center = v - jnp.mean(v, axis=-1, keepdims=True)
    spread = jnp.mean(center * center, axis=-1, keepdims=True)
    return center * lax.rsqrt(spread + 1e-05)


def iota(shape, dim):
    return lax.broadcasted_iota(jnp.int32, shape, dim)


def rows(start, size):
    return pl.ds(pl.multiple_of(start, 16), size)


def kernel(
    x_hbm,
    sv_hbm,
    w_hbm,
    wf_hbm,
    fl_hbm,
    out_hbm,
    sr_hbm,
    xraw,
    edge,
    side,
    xq,
    xkv,
    wt,
    wft,
    flb,
    vb,
    svz,
    svr,
    cst,
    xc,
    qkvc,
    osc,
    sbuf,
    rbuf,
    wsc,
    csc,
    sr_v,
    kc,
    vc,
    q_s,
    k_s,
    v_s,
    bias,
    mix,
    obuf,
    load_sem,
    halo_s,
    halo_r,
    flag_s,
    flag_r,
    y_s,
    y_r,
    x_s,
    x_r,
    d_s,
    d_r,
    cz_s,
    cz_r,
    cr_s,
    cr_r,
    p_s,
    p_r,
    o_s,
):
    img = lax.axis_index("img")
    r = lax.axis_index("row")
    c = lax.axis_index("col")
    y = r // 4
    xl = (r // 2) % 2
    core = r % 2
    up, down = (r + 15) % 16, (r + 1) % 16
    left, right = (c + 15) % 16, (c + 1) % 16
    dev_y = [(img, ((y + k) % 4) * 4 + xl * 2 + core, c) for k in (1, 3)]
    dev_p = (img, y * 4 + xl * 2 + (1 - core), c)
    dev_x = [(k, y * 4 + (1 - xl) * 2 + core, c) for k in (1 - img, img)]

    def local(src, dst, i):
        return pltpu.make_async_copy(src, dst, load_sem.at[i])

    def remote(src, dst, s, t, dev):
        return pltpu.make_async_remote_copy(
            src_ref=src, dst_ref=dst, send_sem=s, recv_sem=t, device_id=dev, device_id_type=MESH
        )

    ld_x = local(x_hbm, xraw.at[pl.ds(128, TOK)], 0)
    ld_w = local(w_hbm, wt.at[rows(r * 144, 144)], 1)
    ld_wf = local(wf_hbm, wft.at[rows(r * PIECE, PIECE)], 2)
    ld_f = local(fl_hbm, flb.at[4], 3)
    ld_z = local(sv_hbm, svz.at[c], 4)
    ld_r = local(sv_hbm, svr.at[r], 5)
    for cp in (ld_x, ld_w, ld_wf, ld_f, ld_z, ld_r):
        cp.start()

    barrier = pltpu.get_barrier_semaphore()

    def greet(dev):
        pl.semaphore_signal(barrier, inc=1, device_id=dev, device_id_type=MESH)

    for i in range(1, 16):
        greet((img, r, (c + i) % 16))
    for i in range(1, 16):
        greet((img, (r + i) % 16, c))
    for rr in (up, down):
        for cc in (left, right):
            greet((img, rr, cc))
    greet(dev_x[0])

    ld_w.wait()
    ld_wf.wait()
    pl.semaphore_wait(barrier, 35)

    def piece(rr, p):
        if p < 3:
            return wt.at[rows(rr * 144 + PIECE * p, PIECE)]
        return wft.at[rows(rr * PIECE, PIECE)]

    def unit(j, column, kernel_core):
        return ((y + (0, 3, 1, 2)[j]) % 4) * 4 + column * 2 + kernel_core

    def mine(j):
        return unit(j, xl, core)

    def y_copy(k, p):
        origin = mine(0) if k < 2 else mine(1 if p % 2 == 0 else 2)
        up_y = k == 0 or (k == 2 and p % 2 == 0)
        to = dev_y[0] if up_y else dev_y[1]
        return remote(piece(origin, p), piece(origin, p), y_s.at[k, p], y_r.at[k, p], to)

    def x_copy(j, p):
        ref = piece(mine(j), p)
        return remote(ref, ref, x_s.at[j, p], x_r.at[j, p], dev_x[p % 2 if p < 3 or j > 1 else 0])

    def d_copy(j, p):
        ref = piece(unit(j % 4, xl if j < 4 else 1 - xl, core), p)
        return remote(ref, ref, d_s.at[j, p], d_r.at[j, p], dev_p)

    def send_own(p):
        y_copy(0, p).start()
        y_copy(1, p).start()
        x_copy(0, p).start()
        d_copy(0, p).start()

    def on_y(k, p):
        y_copy(k, p).wait_recv()
        if k == p % 2:
            y_copy(2, p).start()
        x_copy(k + 1, p).start()
        d_copy(k + 1, p).start()

    def on_x(j, p):
        x_copy(j, p).wait_recv()
        d_copy(4 + j, p).start()

    def first(p):
        on_y(0, p)
        on_y(1, p)
        on_x(0, p)

    def second(p):
        on_y(2, p)
        on_x(1, p)
        on_x(2, p)

    for p in range(3):
        send_own(p)

    ld_x.wait()
    pick = iota((64, 256), 0)
    at = (pick % 32) // 4 * 32 + pick % 4 + (pick // 32) * 28
    pick = (iota((64, 256), 1) == at).astype(BF)
    for g in range(4):
        both = nn(pick, xraw[128 + 256 * g : 384 + 256 * g]).astype(BF)
        edge[32 * g : 32 * g + 32] = both[:32]
        edge[128 + 32 * g : 160 + 32 * g] = both[32:]

    def halo(i, src, dst, dev):
        return remote(src, dst, halo_s.at[i], halo_r.at[i], dev)

    e_l, e_r = 0, 128
    halos = [
        halo(0, x_hbm.at[pl.ds(0, 128)], xraw.at[pl.ds(1152, 128)], (img, up, c)),
        halo(1, x_hbm.at[pl.ds(896, 128)], xraw.at[pl.ds(0, 128)], (img, down, c)),
        halo(2, edge.at[pl.ds(e_l, 128)], side.at[1, pl.ds(16, 128)], (img, r, left)),
        halo(3, edge.at[pl.ds(e_r, 128)], side.at[0, pl.ds(16, 128)], (img, r, right)),
        halo(4, edge.at[pl.ds(e_l, 16)], side.at[1, pl.ds(144, 16)], (img, up, left)),
        halo(5, edge.at[pl.ds(e_r, 16)], side.at[0, pl.ds(144, 16)], (img, up, right)),
        halo(6, edge.at[pl.ds(e_l + 112, 16)], side.at[1, pl.ds(0, 16)], (img, down, left)),
        halo(7, edge.at[pl.ds(e_r + 112, 16)], side.at[0, pl.ds(0, 16)], (img, down, right)),
    ]
    for cp in halos:
        cp.start()
    flags = []
    for dy, rr in ((-1, up), (0, r), (1, down)):
        for dx, cc in ((-1, left), (0, c), (1, right)):
            if dy or dx:
                to = (1 - dy) * 3 + (1 - dx)
                flags.append(remote(fl_hbm, flb.at[to], flag_s.at[to], flag_r.at[to], (img, rr, cc)))
    for cp in flags:
        cp.start()
    carriers = []
    for i in range(1, 16):
        dev = (img, r, (c + i) % 16)
        carriers.append(remote(sv_hbm, svz.at[c], cz_s.at[i], cz_r.at[i], dev))
        dev = (img, (r + i) % 16, c)
        carriers.append(remote(sv_hbm, svr.at[r], cr_s.at[i], cr_r.at[i], dev))
    for cp in carriers:
        cp.start()

    ones32 = jnp.ones((32, 128), BF)
    diag = (iota((32, 32), 0) == iota((32, 32), 1)).astype(F32)
    keep_up = jnp.where(r > 0, 1.0, 0.0)
    keep_down = jnp.where(r < 15, 1.0, 0.0)
    keep_left = jnp.where(c > 0, 1.0, 0.0)
    keep_right = jnp.where(c < 15, 1.0, 0.0)

    def group(g, dx):
        slot, at, keep = 1, 4 * (g - 1), 1.0
        if g == 0:
            slot, at, keep = 0, 28, keep_up
        if g == 9:
            slot, at, keep = 2, 0, keep_down
        return flb[slot * 3 + 1 + dx][at : at + 4].astype(F32) * keep

    def center_flags(g):
        f = group(g, 0)
        spread = [jnp.broadcast_to(f[i : i + 1], (32, 32)) * diag for i in range(4)]
        spread = jnp.concatenate(spread, axis=0).astype(BF)
        vb[128 * g : 128 * g + 128] = nn(spread, ones32).astype(BF)

    def side_flags(g, dx):
        f = group(g, dx) * (keep_left if dx < 0 else keep_right)
        p = iota((16, 32), 0)
        lane = p % 4 + (28 if dx < 0 else 0)
        spread = jnp.zeros((16, 32), F32)
        for i in range(4):
            spread = spread + jnp.where(p // 4 == i, jnp.broadcast_to(f[i : i + 1], (16, 32)), 0.0)
        spread = jnp.where(iota((16, 32), 1) == lane, spread, 0.0).astype(BF)
        start = CEN + (0 if dx < 0 else SIDE) + 16 * g
        vb[start : start + 16] = nn(spread, ones32).astype(BF)

    def norm_block(ref, src, dst, n, own):
        for i in range(0, n, 32):
            normed = layer_norm(ref[src + i : src + i + 32].astype(F32))
            if own is not None:
                xq[own + i : own + i + 32] = normed.astype(BF)
            mask = vb[dst + i : dst + i + 32].astype(F32)
            normed = normed * jnp.concatenate([mask] * 6, axis=1)
            xkv[dst + i : dst + i + 32] = normed.astype(BF)

    ld_f.wait()
    for g in range(1, 9):
        center_flags(g)

    def own_norm(i):
        norm_block(xraw, 128 + 128 * i, 128 + 128 * i, 128, 128 * i)

    own_norm(0)
    own_norm(1)
    for p in range(3):
        first(p)
        own_norm(2 + p)
    send_own(3)
    for i in range(5, 8):
        own_norm(i)
    second(0)

    for cp in halos:
        cp.wait_recv()
    for cp in flags:
        cp.wait_recv()
    for g in (0, 9):
        center_flags(g)
    for g in range(10):
        side_flags(g, -1)
        side_flags(g, 1)
    norm_block(xraw, 0, 0, 128, None)
    norm_block(xraw, 1152, 1152, 128, None)
    for p in (1, 2):
        second(p)
    norm_block(side.at[0], 0, CEN, SIDE, None)
    norm_block(side.at[1], 0, CEN + SIDE, SIDE, None)
    for p in range(3):
        on_x(3, p)

    ld_z.wait()
    ld_r.wait()
    for cp in carriers:
        cp.wait_recv()
    for p in range(16):
        for i in range(2):
            cst[4 * p + 2 * i : 4 * p + 2 * i + 2] = svz[p, i].astype(F32)
            cst[64 + 4 * p + 2 * i : 66 + 4 * p + 2 * i] = svr[p, i].astype(F32)
    for i in range(4):
        xc[32 * i : 32 * i + 32] = layer_norm(cst[32 * i : 32 * i + 32]).astype(BF)

    qi = iota((256, 512), 0) % 128
    ki = iota((256, 512), 1)
    q_row, q_col = qi // 32, qi % 32
    in_side = ki >= 384
    k2 = jnp.where(ki >= 432, ki - 432, ki - 384)
    k_row = jnp.where(in_side, k2 // 4, ki // 32)
    k_col = jnp.where(in_side, k2 % 4 + jnp.where(ki >= 432, 36, 0), ki % 32 + 4)
    dr, dc = k_row - q_row, k_col - q_col
    near = (ki < 480) & (dr >= 0) & (dr <= 8) & (dc >= 0) & (dc <= 8)
    for wr in range(2):
        seen = near | (ki == 480 + wr * 2 + q_col // 16)
        bias[wr] = jnp.where(seen, 0.0, MASKED)

    for j in range(8):
        for p in range(3):
            d_copy(j, p).wait_recv()


    def carrier_qkv(n, carry):
        got = nt(xc[...], wt[rows(n * 256, 256)])
        qkvc[:, pl.ds(pl.multiple_of(n * 256, 256), 256)] = got.astype(BF)
        return carry

    lax.fori_loop(0, 9, carrier_qkv, 0)
    first(3)
    low = iota((64, 128), 1) < 64
    lane64 = iota((64, 128), 1)
    zero = jnp.zeros((64, 128), BF)
    m_stat = jnp.zeros((64, 128), F32)
    l_stat = jnp.ones((64, 128), F32)
    for j in range(PAIRS):
        qp = qkvc[64:128, 128 * j : 128 * j + 128]
        kp = qkvc[0:64, D + 128 * j : D + 128 * j + 128]
        vp = qkvc[0:64, 2 * D + 128 * j : 2 * D + 128 * j + 128]
        qs = jnp.concatenate([jnp.where(low, qp, zero), jnp.where(low, zero, qp)], axis=0)
        sc = nt(qs, kp) * 0.125
        m = jnp.max(sc, axis=-1, keepdims=True)
        e = jnp.exp(sc - m)
        l = jnp.sum(e, axis=-1, keepdims=True)
        o = nn(e.astype(BF), vp) / l
        osc[:, 128 * j : 128 * j + 128] = jnp.where(low, o[:64], o[64:])
        for k in range(2):
            m_stat = jnp.where(lane64 == 2 * j + k, m[64 * k : 64 * k + 64], m_stat)
            l_stat = jnp.where(lane64 == 2 * j + k, l[64 * k : 64 * k + 64], l_stat)
    osc[:, D : D + 128] = m_stat
    osc[:, D + 128 : D + 256] = l_stat
    for p in range(16):
        sbuf[p] = osc[4 * p : 4 * p + 4]
    rbuf[r] = sbuf[r]
    parts = []
    for i in range(1, 16):
        to = (r + i) % 16
        parts.append(remote(sbuf.at[to], rbuf.at[r], p_s.at[i], p_r.at[i], (img, to, c)))
    for cp in parts:
        cp.start()
    second(3)

    def token_q(n, carry):
        wide = pl.ds(pl.multiple_of(n * 256, 256), 256)
        w_n = wt[rows(n * 256, 256)]
        for i in range(4):
            got = nt(xq[256 * i : 256 * i + 256], w_n)
            q_s[256 * i : 256 * i + 256, wide] = (got * Q_SCALE).astype(BF)
        return carry

    lax.fori_loop(0, 3, token_q, 0)
    on_x(3, 3)

    def token_kv(n, carry):
        wide = pl.ds(pl.multiple_of(n * 256, 256), 256)
        w_k = wt[rows(D + n * 256, 256)]
        w_w = wt[rows(2 * D + n * 256, 256)]
        for i in range(4):
            k_s[400 * i : 400 * i + 400, wide] = nt(xkv[400 * i : 400 * i + 400], w_k).astype(BF)
        for i in range(4):
            v_s[400 * i : 400 * i + 400, wide] = nt(xkv[400 * i : 400 * i + 400], w_w).astype(BF)
        return carry

    lax.fori_loop(0, 3, token_kv, 0)

    for j in range(8):
        d_copy(j, 3).wait_recv()

    for cp in parts:
        cp.wait_recv()
    top = rbuf[0, :, D : D + 128]
    for p in range(1, 16):
        top = jnp.maximum(top, rbuf[p, :, D : D + 128])
    total = jnp.zeros((4, 128), F32)
    for p in range(16):
        total = total + jnp.exp(rbuf[p, :, D : D + 128] - top) * rbuf[p, :, D + 128 : D + 256]
    for p in range(16):
        share = jnp.exp(rbuf[p, :, D : D + 128] - top) * rbuf[p, :, D + 128 : D + 256]
        wsc[4 * p : 4 * p + 4] = share / total
    widen = (iota((128, D), 0) == iota((128, D), 1) // 64).astype(F32)
    wide_share = jnp.dot(
        wsc[...], widen, preferred_element_type=F32, precision=lax.Precision.HIGHEST
    )
    joined = jnp.zeros((4, D), F32)
    for p in range(16):
        joined = joined + wide_share[4 * p : 4 * p + 4] * rbuf[p, :, 0:D]
    csc[...] = jnp.zeros((2, 32, D), F32)
    csc[0, 0:4] = joined
    csc[1, 0:2] = svr[r, 0].astype(F32)
    csc[1, 2:4] = svr[r, 1].astype(F32)
    renewed = csc[1] + nt(csc[0].astype(BF), wft[...])
    sr_v[0] = renewed[0:2].astype(BF)
    sr_v[1] = renewed[2:4].astype(BF)
    st_sr = pltpu.make_async_copy(sr_v, sr_hbm, load_sem.at[6])
    st_sr.start()
    again = layer_norm(renewed).astype(BF)
    kc[...] = nt(again, wt[D : 2 * D]).astype(BF)
    vc[...] = nt(again, wt[2 * D : 3 * D]).astype(BF)

    low128 = iota((128, 128), 1) < 64
    zero128 = jnp.zeros((128, 128), BF)
    ones_c = jnp.ones((32, 128), BF)

    def tile(t, carry):
        cen = rows(128 * t, 384)
        lef = rows(CEN + 16 * t, 48)
        rig = rows(CEN + SIDE + 16 * t, 48)
        here = rows(128 * t, 128)
        seen = bias.at[t // 4]
        vbt = jnp.concatenate([vb[cen], vb[lef], vb[rig], ones_c], axis=0)
        for j in range(PAIRS):
            ln = pl.ds(128 * j, 128)
            kt = jnp.concatenate([k_s[cen, ln], k_s[lef, ln], k_s[rig, ln], kc[:, ln]], axis=0)
            vt = jnp.concatenate([v_s[cen, ln], v_s[lef, ln], v_s[rig, ln], vc[:, ln]], axis=0)
            qp = q_s[here, ln]
            qs = jnp.concatenate(
                [jnp.where(low128, qp, zero128), jnp.where(low128, zero128, qp)], axis=0
            )
            sc = nt(qs, kt) + seen[...]
            m = jnp.max(sc, axis=-1, keepdims=True)
            e = jnp.exp2(sc - m).astype(BF)
            o = nn(e, jnp.concatenate([vt, vbt], axis=1))
            o = o[:, :128] / o[:, 128:]
            mix[here, ln] = jnp.where(low128, o[:128], o[128:]).astype(BF)
        return carry

    lax.fori_loop(0, 8, tile, 0)

    outs = []
    for i in range(4):
        mine_rows = pl.ds(256 * i, 256)
        added = nt(mix[256 * i : 256 * i + 256], wft[...])
        got = xraw[128 + 256 * i : 384 + 256 * i].astype(F32) + added
        obuf[i] = got.astype(BF)
        cp = pltpu.make_async_copy(obuf.at[i], out_hbm.at[mine_rows], o_s.at[i])
        cp.start()
        outs.append(cp)

    for cp in outs:
        cp.wait()
    st_sr.wait()
    for cp in halos + flags + carriers + parts:
        cp.wait_send()
    for p in range(4):
        for k in range(3):
            y_copy(k, p).wait_send()
        for j in range(4):
            x_copy(j, p).wait_send()
        for j in range(8):
            d_copy(j, p).wait_send()


def local(grid_elements, summary_vectors, triple_projection, final_projection, genuine_flags):
    any_spec = pl.BlockSpec(memory_space=pl.ANY)
    dma = pltpu.SemaphoreType.DMA
    out, summary = pl.pallas_call(
        kernel,
        out_shape=(
            jax.ShapeDtypeStruct((TOK, D), BF),
            jax.ShapeDtypeStruct((2, 2, D), BF),
        ),
        in_specs=[any_spec] * 5,
        out_specs=(any_spec, any_spec),
        scratch_shapes=[
            pltpu.VMEM((CEN, D), BF),
            pltpu.VMEM((256, D), BF),
            pltpu.VMEM((2, SIDE, D), BF),
            pltpu.VMEM((TOK, D), BF),
            pltpu.VMEM((KEYS, D), BF),
            pltpu.VMEM((3 * D, D), BF),
            pltpu.VMEM((D, D), BF),
            pltpu.VMEM((9, 32, 32), jnp.int32),
            pltpu.VMEM((KEYS, 128), BF),
            pltpu.VMEM((16, 2, 2, D), BF),
            pltpu.VMEM((16, 2, 2, D), BF),
            pltpu.VMEM((128, D), F32),
            pltpu.VMEM((128, D), BF),
            pltpu.VMEM((128, 3 * D), BF),
            pltpu.VMEM((64, 1024), F32),
            pltpu.VMEM((16, 4, 1024), F32),
            pltpu.VMEM((16, 4, 1024), F32),
            pltpu.VMEM((64, 128), F32),
            pltpu.VMEM((2, 32, D), F32),
            pltpu.VMEM((2, 2, D), BF),
            pltpu.VMEM((32, D), BF),
            pltpu.VMEM((32, D), BF),
            pltpu.VMEM((TOK, D), BF),
            pltpu.VMEM((KEYS, D), BF),
            pltpu.VMEM((KEYS, D), BF),
            pltpu.VMEM((2, 256, 512), F32),
            pltpu.VMEM((TOK, D), BF),
            pltpu.VMEM((4, 256, D), BF),
            dma((7,)),
            dma((8,)),
            dma((8,)),
            dma((9,)),
            dma((9,)),
            dma((3, 4)),
            dma((3, 4)),
            dma((4, 4)),
            dma((4, 4)),
            dma((8, 4)),
            dma((8, 4)),
            dma((16,)),
            dma((16,)),
            dma((16,)),
            dma((16,)),
            dma((16,)),
            dma((16,)),
            dma((4,)),
        ],
        compiler_params=pltpu.CompilerParams(
            collective_id=0, has_side_effects=True, vmem_limit_bytes=60 * 1024 * 1024
        ),
        name="block",
    )(
        grid_elements.reshape(TOK, D),
        summary_vectors,
        triple_projection.T,
        final_projection.T,
        genuine_flags,
    )
    return out.reshape(grid_elements.shape), summary


def solution(mesh):
    placed = (
        P(("img", "row"), "col", None),
        P(("img", "row"), "col", None),
        P(None, "row"),
        P(None, "row"),
        P(("img", "row"), "col"),
    )
    return jax.shard_map(
        local,
        mesh=mesh,
        in_specs=placed,
        out_specs=(P(("img", "row"), "col", None), P(("img", "row"), "col", None)),
        check_vma=False,
    )
```

```python
import functools
import math

import jax
import jax.numpy as jnp
from jax import lax
from jax.experimental import pallas as pl
from jax.experimental.pallas import tpu as pltpu
from jax.sharding import PartitionSpec as P

MESH = pl.DeviceIdType.MESH
D = 768
HEADS = 12
PAIRS = HEADS // 2
TOK = 1024
CEN = 1280
SIDE = 160
KEYS = CEN + 2 * SIDE
PIECE = 48
F32 = jnp.float32
BF = jnp.bfloat16
NT = (((1,), (1,)), ((), ()))
Q_SCALE = 0.125 * math.log2(math.e)
MASKED = -1e30


def nt(a, b):
    return lax.dot_general(a, b, NT, preferred_element_type=F32)


def nn(a, b):
    return jnp.dot(a, b, preferred_element_type=F32)


def layer_norm(v):
    center = v - jnp.mean(v, axis=-1, keepdims=True)
    spread = jnp.mean(center * center, axis=-1, keepdims=True)
    return center * lax.rsqrt(spread + 1e-05)


def iota(shape, dim):
    return lax.broadcasted_iota(jnp.int32, shape, dim)


def rows(start, size):
    return pl.ds(pl.multiple_of(start, 16), size)


def kernel(
    x_hbm,
    sv_hbm,
    w_hbm,
    wf_hbm,
    fl_hbm,
    out_hbm,
    sr_hbm,
    xraw,
    edge,
    side,
    xq,
    xkv,
    wt,
    wft,
    flb,
    vb,
    svz,
    svr,
    cst,
    xc,
    qkvc,
    osc,
    sbuf,
    rbuf,
    wsc,
    csc,
    sr_v,
    kc,
    vc,
    q_s,
    k_s,
    v_s,
    bias,
    mix,
    obuf,
    load_sem,
    halo_s,
    halo_r,
    flag_s,
    flag_r,
    y_s,
    y_r,
    x_s,
    x_r,
    d_s,
    d_r,
    cz_s,
    cz_r,
    cr_s,
    cr_r,
    p_s,
    p_r,
    o_s,
):
    img = lax.axis_index("img")
    r = lax.axis_index("row")
    c = lax.axis_index("col")
    y = r // 4
    xl = (r // 2) % 2
    core = r % 2
    up, down = (r + 15) % 16, (r + 1) % 16
    left, right = (c + 15) % 16, (c + 1) % 16
    dev_y = [(img, ((y + k) % 4) * 4 + xl * 2 + core, c) for k in (1, 3)]
    dev_p = (img, y * 4 + xl * 2 + (1 - core), c)
    dev_x = [(k, y * 4 + (1 - xl) * 2 + core, c) for k in (1 - img, img)]

    def local(src, dst, i):
        return pltpu.make_async_copy(src, dst, load_sem.at[i])

    def remote(src, dst, s, t, dev):
        return pltpu.make_async_remote_copy(
            src_ref=src, dst_ref=dst, send_sem=s, recv_sem=t, device_id=dev, device_id_type=MESH
        )

    ld_x = local(x_hbm, xraw.at[pl.ds(128, TOK)], 0)
    ld_w = local(w_hbm, wt.at[rows(r * 144, 144)], 1)
    ld_wf = local(wf_hbm, wft.at[rows(r * PIECE, PIECE)], 2)
    ld_f = local(fl_hbm, flb.at[4], 3)
    ld_z = local(sv_hbm, svz.at[c], 4)
    ld_r = local(sv_hbm, svr.at[r], 5)
    for cp in (ld_x, ld_w, ld_wf, ld_f, ld_z, ld_r):
        cp.start()

    barrier = pltpu.get_barrier_semaphore()

    def greet(dev):
        pl.semaphore_signal(barrier, inc=1, device_id=dev, device_id_type=MESH)

    for i in range(1, 16):
        greet((img, r, (c + i) % 16))
    for i in range(1, 16):
        greet((img, (r + i) % 16, c))
    for rr in (up, down):
        for cc in (left, right):
            greet((img, rr, cc))
    greet(dev_x[0])

    ld_w.wait()
    ld_wf.wait()
    pl.semaphore_wait(barrier, 35)

    def piece(rr, p):
        if p < 3:
            return wt.at[rows(rr * 144 + PIECE * p, PIECE)]
        return wft.at[rows(rr * PIECE, PIECE)]

    def unit(j, column, kernel_core):
        return ((y + (0, 3, 1, 2)[j]) % 4) * 4 + column * 2 + kernel_core

    def mine(j):
        return unit(j, xl, core)

    def y_copy(k, p):
        origin = mine(0) if k < 2 else mine(1 if p % 2 == 0 else 2)
        up_y = k == 0 or (k == 2 and p % 2 == 0)
        to = dev_y[0] if up_y else dev_y[1]
        return remote(piece(origin, p), piece(origin, p), y_s.at[k, p], y_r.at[k, p], to)

    def x_copy(j, p):
        ref = piece(mine(j), p)
        return remote(ref, ref, x_s.at[j, p], x_r.at[j, p], dev_x[p % 2 if p < 3 or j > 1 else 0])

    def d_copy(j, p):
        ref = piece(unit(j % 4, xl if j < 4 else 1 - xl, core), p)
        return remote(ref, ref, d_s.at[j, p], d_r.at[j, p], dev_p)

    def send_own(p):
        y_copy(0, p).start()
        y_copy(1, p).start()
        x_copy(0, p).start()
        d_copy(0, p).start()

    def on_y(k, p):
        y_copy(k, p).wait_recv()
        if k == p % 2:
            y_copy(2, p).start()
        x_copy(k + 1, p).start()
        d_copy(k + 1, p).start()

    def on_x(j, p):
        x_copy(j, p).wait_recv()
        d_copy(4 + j, p).start()

    def first(p):
        on_y(0, p)
        on_y(1, p)
        on_x(0, p)

    def second(p):
        on_y(2, p)
        on_x(1, p)
        on_x(2, p)

    for p in range(3):
        send_own(p)

    ld_x.wait()
    pick = iota((64, 256), 0)
    at = (pick % 32) // 4 * 32 + pick % 4 + (pick // 32) * 28
    pick = (iota((64, 256), 1) == at).astype(BF)
    for g in range(4):
        both = nn(pick, xraw[128 + 256 * g : 384 + 256 * g]).astype(BF)
        edge[32 * g : 32 * g + 32] = both[:32]
        edge[128 + 32 * g : 160 + 32 * g] = both[32:]

    def halo(i, src, dst, dev):
        return remote(src, dst, halo_s.at[i], halo_r.at[i], dev)

    e_l, e_r = 0, 128
    halos = [
        halo(0, x_hbm.at[pl.ds(0, 128)], xraw.at[pl.ds(1152, 128)], (img, up, c)),
        halo(1, x_hbm.at[pl.ds(896, 128)], xraw.at[pl.ds(0, 128)], (img, down, c)),
        halo(2, edge.at[pl.ds(e_l, 128)], side.at[1, pl.ds(16, 128)], (img, r, left)),
        halo(3, edge.at[pl.ds(e_r, 128)], side.at[0, pl.ds(16, 128)], (img, r, right)),
        halo(4, edge.at[pl.ds(e_l, 16)], side.at[1, pl.ds(144, 16)], (img, up, left)),
        halo(5, edge.at[pl.ds(e_r, 16)], side.at[0, pl.ds(144, 16)], (img, up, right)),
        halo(6, edge.at[pl.ds(e_l + 112, 16)], side.at[1, pl.ds(0, 16)], (img, down, left)),
        halo(7, edge.at[pl.ds(e_r + 112, 16)], side.at[0, pl.ds(0, 16)], (img, down, right)),
    ]
    for cp in halos:
        cp.start()
    flags = []
    for dy, rr in ((-1, up), (0, r), (1, down)):
        for dx, cc in ((-1, left), (0, c), (1, right)):
            if dy or dx:
                to = (1 - dy) * 3 + (1 - dx)
                flags.append(remote(fl_hbm, flb.at[to], flag_s.at[to], flag_r.at[to], (img, rr, cc)))
    for cp in flags:
        cp.start()
    carriers = []
    for i in range(1, 16):
        dev = (img, r, (c + i) % 16)
        carriers.append(remote(sv_hbm, svz.at[c], cz_s.at[i], cz_r.at[i], dev))
        dev = (img, (r + i) % 16, c)
        carriers.append(remote(sv_hbm, svr.at[r], cr_s.at[i], cr_r.at[i], dev))
    for cp in carriers:
        cp.start()

    ones32 = jnp.ones((32, 128), BF)
    diag = (iota((32, 32), 0) == iota((32, 32), 1)).astype(F32)
    keep_up = jnp.where(r > 0, 1.0, 0.0)
    keep_down = jnp.where(r < 15, 1.0, 0.0)
    keep_left = jnp.where(c > 0, 1.0, 0.0)
    keep_right = jnp.where(c < 15, 1.0, 0.0)

    def group(g, dx):
        slot, at, keep = 1, 4 * (g - 1), 1.0
        if g == 0:
            slot, at, keep = 0, 28, keep_up
        if g == 9:
            slot, at, keep = 2, 0, keep_down
        return flb[slot * 3 + 1 + dx][at : at + 4].astype(F32) * keep

    def center_flags(g):
        f = group(g, 0)
        spread = [jnp.broadcast_to(f[i : i + 1], (32, 32)) * diag for i in range(4)]
        spread = jnp.concatenate(spread, axis=0).astype(BF)
        vb[128 * g : 128 * g + 128] = nn(spread, ones32).astype(BF)

    def side_flags(g, dx):
        f = group(g, dx) * (keep_left if dx < 0 else keep_right)
        p = iota((16, 32), 0)
        lane = p % 4 + (28 if dx < 0 else 0)
        spread = jnp.zeros((16, 32), F32)
        for i in range(4):
            spread = spread + jnp.where(p // 4 == i, jnp.broadcast_to(f[i : i + 1], (16, 32)), 0.0)
        spread = jnp.where(iota((16, 32), 1) == lane, spread, 0.0).astype(BF)
        start = CEN + (0 if dx < 0 else SIDE) + 16 * g
        vb[start : start + 16] = nn(spread, ones32).astype(BF)

    def norm_block(ref, src, dst, n, own):
        for i in range(0, n, 32):
            normed = layer_norm(ref[src + i : src + i + 32].astype(F32))
            if own is not None:
                xq[own + i : own + i + 32] = normed.astype(BF)
            mask = vb[dst + i : dst + i + 32].astype(F32)
            normed = normed * jnp.concatenate([mask] * 6, axis=1)
            xkv[dst + i : dst + i + 32] = normed.astype(BF)

    ld_f.wait()
    for g in range(1, 9):
        center_flags(g)

    def own_norm(i):
        norm_block(xraw, 128 + 128 * i, 128 + 128 * i, 128, 128 * i)

    own_norm(0)
    own_norm(1)
    for p in range(3):
        first(p)
        own_norm(2 + p)
    send_own(3)
    for i in range(5, 8):
        own_norm(i)
    second(0)

    for cp in halos:
        cp.wait_recv()
    for cp in flags:
        cp.wait_recv()
    for g in (0, 9):
        center_flags(g)
    for g in range(10):
        side_flags(g, -1)
        side_flags(g, 1)
    norm_block(xraw, 0, 0, 128, None)
    norm_block(xraw, 1152, 1152, 128, None)
    for p in (1, 2):
        second(p)
    norm_block(side.at[0], 0, CEN, SIDE, None)
    norm_block(side.at[1], 0, CEN + SIDE, SIDE, None)
    for j in (0, 1, 2, 4, 5, 6):
        for p in range(3):
            d_copy(j, p).wait_recv()

    def columns(ref, out, step, many, w_at, at, width, scale):
        w_n = wt[w_at : w_at + width]
        for i in range(many):
            got = nt(ref[step * i : step * i + step], w_n)
            if scale is not None:
                got = got * scale
            out[step * i : step * i + step, at : at + width] = got.astype(BF)

    def half(which, early=False):
        @pl.when(which == 0)
        def _():
            for n in range(3):
                columns(xq, q_s, 256, 4, 256 * n, 256 * n, 256, Q_SCALE)
                if early:
                    on_x(3, n)
            columns(xkv, k_s, 400, 4, D, 0, 256, None)
            columns(xkv, k_s, 400, 4, D + 256, 256, 128, None)

        @pl.when(which == 1)
        def _():
            columns(xkv, k_s, 400, 4, D + 384, 384, 128, None)
            for n in range(3):
                columns(xkv, v_s, 400, 4, 2 * D + 256 * n, 256 * n, 256, None)
                if early:
                    on_x(3, n)
            columns(xkv, k_s, 400, 4, D + 512, 512, 256, None)

    half(y // 2, True)

    ld_z.wait()
    ld_r.wait()
    for cp in carriers:
        cp.wait_recv()
    for p in range(16):
        for i in range(2):
            cst[4 * p + 2 * i : 4 * p + 2 * i + 2] = svz[p, i].astype(F32)
            cst[64 + 4 * p + 2 * i : 66 + 4 * p + 2 * i] = svr[p, i].astype(F32)
    for i in range(4):
        xc[32 * i : 32 * i + 32] = layer_norm(cst[32 * i : 32 * i + 32]).astype(BF)

    qi = iota((256, 512), 0) % 128
    ki = iota((256, 512), 1)
    q_row, q_col = qi // 32, qi % 32
    in_side = ki >= 384
    k2 = jnp.where(ki >= 432, ki - 432, ki - 384)
    k_row = jnp.where(in_side, k2 // 4, ki // 32)
    k_col = jnp.where(in_side, k2 % 4 + jnp.where(ki >= 432, 36, 0), ki % 32 + 4)
    dr, dc = k_row - q_row, k_col - q_col
    near = (ki < 480) & (dr >= 0) & (dr <= 8) & (dc >= 0) & (dc <= 8)
    for wr in range(2):
        seen = near | (ki == 480 + wr * 2 + q_col // 16)
        bias[wr] = jnp.where(seen, 0.0, MASKED)

    for j in (3, 7):
        for p in range(3):
            d_copy(j, p).wait_recv()

    def carrier_qkv(n, carry):
        got = nt(xc[...], wt[rows(n * 256, 256)])
        qkvc[:, pl.ds(pl.multiple_of(n * 256, 256), 256)] = got.astype(BF)
        return carry

    lax.fori_loop(0, 9, carrier_qkv, 0)
    first(3)
    low = iota((64, 128), 1) < 64
    lane64 = iota((64, 128), 1)
    zero = jnp.zeros((64, 128), BF)
    m_stat = jnp.zeros((64, 128), F32)
    l_stat = jnp.ones((64, 128), F32)
    for j in range(PAIRS):
        qp = qkvc[64:128, 128 * j : 128 * j + 128]
        kp = qkvc[0:64, D + 128 * j : D + 128 * j + 128]
        vp = qkvc[0:64, 2 * D + 128 * j : 2 * D + 128 * j + 128]
        qs = jnp.concatenate([jnp.where(low, qp, zero), jnp.where(low, zero, qp)], axis=0)
        sc = nt(qs, kp) * 0.125
        m = jnp.max(sc, axis=-1, keepdims=True)
        e = jnp.exp(sc - m)
        l = jnp.sum(e, axis=-1, keepdims=True)
        o = nn(e.astype(BF), vp) / l
        osc[:, 128 * j : 128 * j + 128] = jnp.where(low, o[:64], o[64:])
        for k in range(2):
            m_stat = jnp.where(lane64 == 2 * j + k, m[64 * k : 64 * k + 64], m_stat)
            l_stat = jnp.where(lane64 == 2 * j + k, l[64 * k : 64 * k + 64], l_stat)
    osc[:, D : D + 128] = m_stat
    osc[:, D + 128 : D + 256] = l_stat
    for p in range(16):
        sbuf[p] = osc[4 * p : 4 * p + 4]
    rbuf[r] = sbuf[r]
    parts = []
    for i in range(1, 16):
        to = (r + i) % 16
        parts.append(remote(sbuf.at[to], rbuf.at[r], p_s.at[i], p_r.at[i], (img, to, c)))
    for cp in parts:
        cp.start()
    second(3)

    half(1 - y // 2)
    on_x(3, 3)

    for j in range(8):
        d_copy(j, 3).wait_recv()

    for cp in parts:
        cp.wait_recv()
    top = rbuf[0, :, D : D + 128]
    for p in range(1, 16):
        top = jnp.maximum(top, rbuf[p, :, D : D + 128])
    total = jnp.zeros((4, 128), F32)
    for p in range(16):
        total = total + jnp.exp(rbuf[p, :, D : D + 128] - top) * rbuf[p, :, D + 128 : D + 256]
    for p in range(16):
        share = jnp.exp(rbuf[p, :, D : D + 128] - top) * rbuf[p, :, D + 128 : D + 256]
        wsc[4 * p : 4 * p + 4] = share / total
    widen = (iota((128, D), 0) == iota((128, D), 1) // 64).astype(F32)
    wide_share = jnp.dot(
        wsc[...], widen, preferred_element_type=F32, precision=lax.Precision.HIGHEST
    )
    joined = jnp.zeros((4, D), F32)
    for p in range(16):
        joined = joined + wide_share[4 * p : 4 * p + 4] * rbuf[p, :, 0:D]
    csc[...] = jnp.zeros((2, 32, D), F32)
    csc[0, 0:4] = joined
    csc[1, 0:2] = svr[r, 0].astype(F32)
    csc[1, 2:4] = svr[r, 1].astype(F32)
    renewed = csc[1] + nt(csc[0].astype(BF), wft[...])
    sr_v[0] = renewed[0:2].astype(BF)
    sr_v[1] = renewed[2:4].astype(BF)
    st_sr = pltpu.make_async_copy(sr_v, sr_hbm, load_sem.at[6])
    st_sr.start()
    again = layer_norm(renewed).astype(BF)
    kc[...] = nt(again, wt[D : 2 * D]).astype(BF)
    vc[...] = nt(again, wt[2 * D : 3 * D]).astype(BF)

    low128 = iota((128, 128), 1) < 64
    zero128 = jnp.zeros((128, 128), BF)
    ones_c = jnp.ones((32, 128), BF)

    def tile(t, carry):
        cen = rows(128 * t, 384)
        lef = rows(CEN + 16 * t, 48)
        rig = rows(CEN + SIDE + 16 * t, 48)
        here = rows(128 * t, 128)
        seen = bias.at[t // 4]
        vbt = jnp.concatenate([vb[cen], vb[lef], vb[rig], ones_c], axis=0)
        for j in range(PAIRS):
            ln = pl.ds(128 * j, 128)
            kt = jnp.concatenate([k_s[cen, ln], k_s[lef, ln], k_s[rig, ln], kc[:, ln]], axis=0)
            vt = jnp.concatenate([v_s[cen, ln], v_s[lef, ln], v_s[rig, ln], vc[:, ln]], axis=0)
            qp = q_s[here, ln]
            qs = jnp.concatenate(
                [jnp.where(low128, qp, zero128), jnp.where(low128, zero128, qp)], axis=0
            )
            sc = nt(qs, kt) + seen[...]
            m = jnp.max(sc, axis=-1, keepdims=True)
            e = jnp.exp2(sc - m).astype(BF)
            o = nn(e, jnp.concatenate([vt, vbt], axis=1))
            o = o[:, :128] / o[:, 128:]
            mix[here, ln] = jnp.where(low128, o[:128], o[128:]).astype(BF)
        return carry

    lax.fori_loop(0, 8, tile, 0)

    outs = []
    for i in range(4):
        mine_rows = pl.ds(256 * i, 256)
        added = nt(mix[256 * i : 256 * i + 256], wft[...])
        got = xraw[128 + 256 * i : 384 + 256 * i].astype(F32) + added
        obuf[i] = got.astype(BF)
        cp = pltpu.make_async_copy(obuf.at[i], out_hbm.at[mine_rows], o_s.at[i])
        cp.start()
        outs.append(cp)

    for cp in outs:
        cp.wait()
    st_sr.wait()
    for cp in halos + flags + carriers + parts:
        cp.wait_send()
    for p in range(4):
        for k in range(3):
            y_copy(k, p).wait_send()
        for j in range(4):
            x_copy(j, p).wait_send()
        for j in range(8):
            d_copy(j, p).wait_send()


def local(grid_elements, summary_vectors, triple_projection, final_projection, genuine_flags):
    any_spec = pl.BlockSpec(memory_space=pl.ANY)
    dma = pltpu.SemaphoreType.DMA
    out, summary = pl.pallas_call(
        kernel,
        out_shape=(
            jax.ShapeDtypeStruct((TOK, D), BF),
            jax.ShapeDtypeStruct((2, 2, D), BF),
        ),
        in_specs=[any_spec] * 5,
        out_specs=(any_spec, any_spec),
        scratch_shapes=[
            pltpu.VMEM((CEN, D), BF),
            pltpu.VMEM((256, D), BF),
            pltpu.VMEM((2, SIDE, D), BF),
            pltpu.VMEM((TOK, D), BF),
            pltpu.VMEM((KEYS, D), BF),
            pltpu.VMEM((3 * D, D), BF),
            pltpu.VMEM((D, D), BF),
            pltpu.VMEM((9, 32, 32), jnp.int32),
            pltpu.VMEM((KEYS, 128), BF),
            pltpu.VMEM((16, 2, 2, D), BF),
            pltpu.VMEM((16, 2, 2, D), BF),
            pltpu.VMEM((128, D), F32),
            pltpu.VMEM((128, D), BF),
            pltpu.VMEM((128, 3 * D), BF),
            pltpu.VMEM((64, 1024), F32),
            pltpu.VMEM((16, 4, 1024), F32),
            pltpu.VMEM((16, 4, 1024), F32),
            pltpu.VMEM((64, 128), F32),
            pltpu.VMEM((2, 32, D), F32),
            pltpu.VMEM((2, 2, D), BF),
            pltpu.VMEM((32, D), BF),
            pltpu.VMEM((32, D), BF),
            pltpu.VMEM((TOK, D), BF),
            pltpu.VMEM((KEYS, D), BF),
            pltpu.VMEM((KEYS, D), BF),
            pltpu.VMEM((2, 256, 512), F32),
            pltpu.VMEM((TOK, D), BF),
            pltpu.VMEM((4, 256, D), BF),
            dma((7,)),
            dma((8,)),
            dma((8,)),
            dma((9,)),
            dma((9,)),
            dma((3, 4)),
            dma((3, 4)),
            dma((4, 4)),
            dma((4, 4)),
            dma((8, 4)),
            dma((8, 4)),
            dma((16,)),
            dma((16,)),
            dma((16,)),
            dma((16,)),
            dma((16,)),
            dma((16,)),
            dma((4,)),
        ],
        compiler_params=pltpu.CompilerParams(
            collective_id=0, has_side_effects=True, vmem_limit_bytes=60 * 1024 * 1024
        ),
        name="block",
    )(
        grid_elements.reshape(TOK, D),
        summary_vectors,
        triple_projection.T,
        final_projection.T,
        genuine_flags,
    )
    return out.reshape(grid_elements.shape), summary


def solution(mesh):
    placed = (
        P(("img", "row"), "col", None),
        P(("img", "row"), "col", None),
        P(None, "row"),
        P(None, "row"),
        P(("img", "row"), "col"),
    )
    return jax.shard_map(
        local,
        mesh=mesh,
        in_specs=placed,
        out_specs=(P(("img", "row"), "col", None), P(("img", "row"), "col", None)),
        check_vma=False,
    )
```
